1024 devices in a mesh: ctx: 16 (over z_hi, x), exp: 64 (over y, z_lo, core).
Axes of the slice: x: 4, y: 8, z: 16 (z_hi: 4, z_lo: 4; z = z_hi * 4 + z_lo), core: 2. Of those that a mesh axis runs over, the one named last changes fastest.
Arguments:
- query: bfloat16 [64, 2048, 2048], P('exp', 'ctx'), may hold values from -8 to 8
- key_value: bfloat16 [64, 2048, 256], P('exp', 'ctx'), may hold values from -8 to 8
- prior_out: bfloat16 [64, 2048, 2048], P('exp', 'ctx'), may hold values from -6 to 6
- prior_lse: float32 [64, 2048, 32], P('exp', 'ctx'), may hold values from 5 to 9
- norm_gain: float32 [2048], replicated, may hold values from 0.25 to 1.75
- w_gate: bfloat16 [64, 2048, 768], P('exp'), may hold values from -0.125 to 0.125
- w_up: bfloat16 [64, 2048, 768], P('exp'), may hold values from -0.125 to 0.125
- expert_ids: int32 [64, 2048, 2], P('exp', 'ctx'), may hold values from 0 to 63, all different within a row; in each aligned block of 128 rows (0 to 127, 128 to 255, ..., all dimensions but the last counted through in order) at most 6 rows name the same one
- route_weight: bfloat16 [64, 2048, 2], P('exp', 'ctx'), may hold values from 0.099609375 to 1
Outputs:
- attended: bfloat16 [64, 2048, 2048], P('exp', 'ctx')
- expert_hidden: bfloat16 [16, 64, 384, 768], P('ctx', 'exp')
The draws below stay inside these ranges and needn't reach their ends.
Inputs may be any that keep to these rules, and one draw needn't show every extreme that they name: `expert_ids`: each token names 2 different experts; the rows of one device name one expert at most 6 times, a bound that some block reaches.
All inputs are finite; a program needn't handle non-finite values.
Results may differ from the reference program's by a relative error of at most 0.0072.
Values may be sent and summed in bfloat16 or wider, within the bound.
No kernel may reach another device: no remote copies, remote signals or barrier semaphores. Data moves between devices by JAX's collectives and lax.ppermute only.
A program may use at most 64 MiB of HBM per device.

```python
import math
import jax
import jax.numpy as jnp
import numpy as np
from jax import lax

HQ = 32
KVH = 2
HD = 64
FF = 768
TOK_DEV = 128
STEPS = 3
IN_FLIGHT = 2
D = 2048
SEQS = 64
SEQLEN = 2048
EXPERTS = 64
CAP = 6
N_CTX = 16


def drawn_fields(key):
    base_key = jax.random.fold_in(key, 4093)
    key_query, key_pairs = jax.random.split(base_key, 2)
    query_shape = (SEQS, SEQLEN, HQ * HD)
    pair_shape = (SEQS, SEQLEN, 2 * KVH * HD)
    queries = jnp.clip(jax.random.normal(key_query, query_shape, jnp.float32), -6.0, 6.0)
    pair_field = jnp.clip(jax.random.normal(key_pairs, pair_shape, jnp.float32), -6.0, 6.0)
    return (queries, pair_field)


def draw_query(key, part):
    return drawn_fields(key)[0].astype(jnp.bfloat16)


def draw_key_value(key, part):
    return drawn_fields(key)[1].astype(jnp.bfloat16)


def block_scale(rng, dims, pieces, low, largest):
    def one(dim, parts):
        heights = jax.random.uniform(jax.random.fold_in(jax.random.fold_in(rng, 6), dim), (parts,), jnp.float32, low / len(pieces), largest / len(pieces))
        return jnp.repeat(jnp.exp(heights), dims[dim] // parts).reshape((-1,) + (1,) * (len(dims) - dim - 1))

    factor_of = one(*pieces[0])
    for cut in pieces[1:]:
        factor_of = factor_of * one(*cut)
    return factor_of


def deal_out(key, own, number, rows, amount, top, bound, skew):
    ranking = jax.random.permutation(key, amount)
    packed, common = load_shares(amount, rows * top, bound, skew, True), load_shares(amount, rows * top, bound, skew, False)
    places = jnp.arange(amount)

    def named(lengths, offset_by):
        used = int((lengths > 0).sum())
        fixed = max(1, used // 4)
        passed = fixed + (places - fixed + offset_by * (used - fixed)) % max(1, amount - fixed)
        return jnp.zeros((amount,), jnp.int32).at[ranking[jnp.where(places < fixed, places, passed)]].set(jnp.asarray(lengths, jnp.int32))

    lengths = jnp.where(number % 4 == 0, named(packed, number // 4), named(common, number - number // 4 - 1))
    mixed = jax.random.permutation(jax.random.fold_in(own, 3), amount)
    giver, receiver = mixed[0:amount // 2 * 2:2], mixed[1:amount // 2 * 2:2]
    margin = jnp.minimum(lengths[giver] - 1, bound - lengths[receiver]) // 2
    margin = jnp.where((giver == ranking[0]) | (receiver == ranking[0]) | (lengths[receiver] == 0), 0, jnp.maximum(margin, 0))
    passed = jax.random.randint(jax.random.fold_in(own, 4), (amount // 2,), 0, 1 << 20) % (margin + 1)
    lengths = lengths.at[giver].add(-passed).at[receiver].add(passed)
    items = jnp.searchsorted(jnp.cumsum(lengths), jnp.arange(rows * top), side="right").astype(jnp.int32)
    table = items.reshape(top, rows).T
    table = table[jax.random.permutation(jax.random.fold_in(own, 1), rows)]
    offset_by = jax.random.randint(jax.random.fold_in(own, 2), (rows, 1), 0, top)
    return jnp.take_along_axis(table, (jnp.arange(top)[None, :] + offset_by) % top, axis=1)


def load_shares(amount, total, reach, slope, full):
    loads = [(1 << 20) // math.isqrt(grade ** slope) + 1 for grade in range(1, amount + 1)]
    largest = reach if full else min(reach, max(-(-total // amount), total * loads[0] // sum(loads)))
    least = 1 if total - largest >= amount - 1 else 0
    given, surplus = [largest] + [least] * (amount - 1), total - largest - least * (amount - 1)
    while surplus > 0:
        free = [i for i in range(1, amount) if given[i] < largest] or [i for i in range(1, amount) if given[i] < reach]
        pool, left = sum([loads[i] for i in free]), surplus
        for i in free:
            more = min(reach - given[i], max(1, left * loads[i] // pool), surplus)
            given[i] = given[i] + more
            surplus = surplus - more
    return np.array(given)


def centred(own_key, extent, width, most, pieces=(), held_as=jnp.bfloat16):
    gain = block_scale(own_key, extent, pieces, -0.22, 0.18) if pieces else 1.0
    values = jax.random.normal(own_key, extent, jnp.float32) * width * gain
    return jnp.minimum(jnp.maximum(values, -most), most).astype(held_as)


def setup_inputs(seed: int = 0) -> dict:
    seeds = jax.random.split(jax.random.key(seed), 10)
    query = draw_query(jax.random.fold_in(seeds[9], 71), 0)
    key_value = draw_key_value(jax.random.fold_in(seeds[9], 71), 0)
    prior_out = centred(seeds[2], (SEQS, SEQLEN, D), 1.0, 6.0, ((0, 64), (1, 16)))
    prior_lse = jnp.clip(5.0 + 4.0 * jax.random.uniform(seeds[3], (SEQS, SEQLEN, HQ), jnp.float32) ** block_scale(seeds[3], (SEQS, SEQLEN, HQ), ((0, 64), (1, 16)), -0.2, 0.2), 5.0, 9.0)
    norm_gain = jnp.clip(1.0 + 0.15 * jax.random.normal(seeds[4], (D,), jnp.float32), 0.25, 1.75)
    w_gate = centred(seeds[5], (EXPERTS, D, FF), D ** -0.5, 0.125, ((0, 64),))
    w_up = centred(seeds[6], (EXPERTS, D, FF), D ** -0.5, 0.125, ((0, 64),))
    expert_ids_keys = jax.random.split(jax.random.fold_in(seeds[7], 1), SEQS * SEQLEN // TOK_DEV)
    expert_ids_turns = jax.random.permutation(jax.random.fold_in(seeds[7], 3), SEQS * SEQLEN // TOK_DEV)
    expert_ids = jax.vmap(lambda own, number: deal_out(jax.random.fold_in(seeds[7], 2), own, number, TOK_DEV, EXPERTS, IN_FLIGHT, CAP, 2))(expert_ids_keys, expert_ids_turns).reshape((SEQS, SEQLEN, IN_FLIGHT))
    route_weight = jnp.clip(jnp.exp(math.log(1.0) - 2.306499 * jax.random.uniform(seeds[8], (SEQS, SEQLEN, IN_FLIGHT), jnp.float32) ** block_scale(seeds[8], (SEQS, SEQLEN, IN_FLIGHT), ((0, 64), (1, 16)), -0.2, 0.2)), 0.099609375, 1.0).astype(jnp.bfloat16)
    return dict(query=query, key_value=key_value, prior_out=prior_out, prior_lse=prior_lse, norm_gain=norm_gain, w_gate=w_gate, w_up=w_up, expert_ids=expert_ids, route_weight=route_weight)


def folded_positions(block_index, row_count, block_total):
    offset = jnp.arange(row_count, dtype=jnp.int32)
    half_rows = row_count // 2
    return jnp.where(offset < half_rows, block_index * half_rows + offset, (2 * block_total - 1 - block_index) * half_rows + offset - half_rows)

def attend_block(queries, window, window_pos, query_pos, prior_rows, prior_logs):
    row_count = queries.shape[0]
    group_size = HQ // KVH
    grouped = queries.astype(jnp.float32).reshape(row_count, KVH, group_size, HD)
    key_rows = window[:, :KVH * HD].astype(jnp.float32).reshape(-1, KVH, HD)
    value_rows = window[:, KVH * HD:].astype(jnp.float32).reshape(-1, KVH, HD)
    scores = jnp.einsum('tgjd,sgd->tgjs', grouped, key_rows) * HD ** (-0.5)
    allowed = (window_pos[None, :] <= query_pos[:, None])[:, None, None, :]
    scores = jnp.where(allowed, scores, -1e+30)
    logs = prior_logs.reshape(row_count, KVH, group_size)
    row_max = jnp.maximum(lax.optimization_barrier(jnp.max(scores, axis=-1)), logs)
    powers = jnp.exp(scores - row_max[..., None])
    carried = jnp.exp(logs - row_max)
    denominator = carried + lax.optimization_barrier(jnp.sum(powers, axis=-1))
    powers_low = lax.optimization_barrier(powers.astype(jnp.bfloat16)).astype(jnp.float32)
    mixed = jnp.einsum('tgjs,sgd->tgjd', powers_low, value_rows)
    earlier = prior_rows.astype(jnp.float32).reshape(row_count, KVH, group_size, HD)
    result = (carried[..., None] * earlier + mixed) / denominator[..., None]
    return result.reshape(row_count, HQ * HD).astype(jnp.bfloat16)

def normalize(row_block, gain_row):
    values = row_block.astype(jnp.float32)
    inverse = lax.rsqrt(lax.optimization_barrier(jnp.mean(values * values, axis=-1, keepdims=True)) + 1e-06)
    return (values * inverse * gain_row).astype(jnp.bfloat16)

def slot_sources(ids_flat, expert_total, capacity):
    assign_total = ids_flat.shape[0]
    onehot = (ids_flat[:, None] == jnp.arange(expert_total, dtype=jnp.int32)[None, :]).astype(jnp.int32)
    before = jnp.cumsum(onehot, axis=0) - onehot
    rank = lax.optimization_barrier(jnp.sum(before * onehot, axis=1))
    slot_of = ids_flat * capacity + rank
    match = slot_of[None, :] == jnp.arange(expert_total * capacity, dtype=jnp.int32)[:, None]
    numbered = jnp.arange(assign_total, dtype=jnp.int32)[None, :] + 1
    return lax.optimization_barrier(jnp.sum(jnp.where(match, numbered, 0), axis=1)) - 1

def reference(query, key_value, prior_out, prior_lse, norm_gain, w_gate, w_up, expert_ids, route_weight):
    seq_total = query.shape[0]
    query_blocks = query.reshape(seq_total, N_CTX, TOK_DEV, HQ * HD)
    pair_blocks = key_value.reshape(seq_total, N_CTX, TOK_DEV, 2 * KVH * HD)
    prior_blocks = prior_out.reshape(seq_total, N_CTX, TOK_DEV, HQ * HD)
    log_blocks = prior_lse.reshape(seq_total, N_CTX, TOK_DEV, HQ)
    step_list = jnp.arange(STEPS, dtype=jnp.int32)

    def block_positions(block_index):
        return folded_positions(block_index, TOK_DEV, N_CTX)

    def one_sequence(sequence):
        pairs_here = pair_blocks[sequence]

        def one_block(block_index, queries, prior_rows, prior_logs):
            sources = (block_index - step_list) % N_CTX
            window = pairs_here[sources].reshape(STEPS * TOK_DEV, 2 * KVH * HD)
            window_pos = jax.vmap(block_positions)(sources).reshape(-1)
            query_pos = block_positions(block_index)
            return attend_block(queries, window, window_pos, query_pos, prior_rows, prior_logs)
        return jax.vmap(one_block)(jnp.arange(N_CTX, dtype=jnp.int32), query_blocks[sequence], prior_blocks[sequence], log_blocks[sequence])
    attended = lax.map(one_sequence, jnp.arange(seq_total, dtype=jnp.int32))
    normed = normalize(attended, norm_gain)
    ids_dev = expert_ids.reshape(seq_total, N_CTX, TOK_DEV * IN_FLIGHT)
    weight_dev = route_weight.reshape(seq_total, N_CTX, TOK_DEV * IN_FLIGHT)

    def table_row(ids_flat):
        return slot_sources(ids_flat, EXPERTS, CAP)
    slot_table = jax.vmap(jax.vmap(table_row))(ids_dev)
    seq_index = jnp.arange(seq_total, dtype=jnp.int32)[None, :, None]
    ctx_index = jnp.arange(N_CTX, dtype=jnp.int32)[:, None, None]

    def expert_block(expert):
        chosen = lax.dynamic_slice_in_dim(slot_table, expert * CAP, CAP, 2)
        chosen = jnp.transpose(chosen, (1, 0, 2))
        filled = chosen >= 0
        clamped = jnp.maximum(chosen, 0)
        row_block = normed[seq_index, ctx_index, clamped // IN_FLIGHT]
        row_block = jnp.where(filled[..., None], row_block, jnp.zeros((), jnp.bfloat16))
        weights = jnp.where(filled, weight_dev[seq_index, ctx_index, clamped], jnp.zeros((), jnp.bfloat16))
        flat_rows = row_block.reshape(-1, HQ * HD)
        gate_out = jnp.dot(flat_rows, w_gate[expert], preferred_element_type=jnp.float32)
        up_out = jnp.dot(flat_rows, w_up[expert], preferred_element_type=jnp.float32)
        hidden = jax.nn.silu(gate_out) * up_out * weights.astype(jnp.float32).reshape(-1)[:, None]
        return hidden.astype(jnp.bfloat16).reshape(N_CTX, seq_total * CAP, FF)
    expert_hidden = lax.map(expert_block, jnp.arange(EXPERTS, dtype=jnp.int32))
    expert_hidden = jnp.transpose(expert_hidden, (1, 0, 2, 3))
    return (attended.reshape(seq_total, N_CTX * TOK_DEV, HQ * HD), expert_hidden)
```

```python
import functools

import jax
import jax.numpy as jnp
from jax import lax
from jax.experimental import pallas as pl
from jax.experimental.pallas import tpu as pltpu
from jax.sharding import PartitionSpec as P

HQ = 32
KVH = 2
HD = 64
FF = 768
D = HQ * HD
TOK = 128
HALF = TOK // 2
EXPERTS = 64
CAP = 6
LANES = 128
MSG_ROWS = 8
MAIN = CAP * D // MSG_ROWS
TAIL = D - MAIN
PAYLOAD = MAIN + LANES
LAST_LANES = (((1,), (1,)), ((), ()))
PAIRS = KVH * 8
QUADS = PAIRS // 2


def iota(shape, dim):
    return lax.broadcasted_iota(jnp.int32, shape, dim)


def as_bf16(mask):
    return jnp.where(mask, 1.0, 0.0).astype(jnp.bfloat16)


def dot_f32(a, b):
    return jnp.dot(a, b, preferred_element_type=jnp.float32)


def dot_t(a, b):
    return lax.dot_general(a, b, LAST_LANES, preferred_element_type=jnp.float32)


def attend_kernel(
    q_ref, kv0_ref, kv1_ref, kv2_ref, prior_ref, lse_ref, gain_ref, ids_ref, rw_ref,
    out_ref, send_ref, kb_ref, vb_ref, lse0_ref, lse1_ref, sq_ref,
):
    block = lax.axis_index("ctx")
    kv_refs = (kv0_ref, kv1_ref, kv2_ref)
    eye = as_bf16(iota((LANES, LANES), 0) == iota((LANES, LANES), 1))
    low = iota((1, LANES), 1) < HALF
    for group in range(KVH):
        first = lse_ref[group * 16 : group * 16 + 8, :]
        second = lse_ref[group * 16 + 8 : group * 16 + 16, :]
        rows = slice(group * 8, group * 8 + 8)
        lse0_ref[rows, :] = jnp.where(low, first, pltpu.roll(second, HALF, 1))
        lse1_ref[rows, :] = jnp.where(low, pltpu.roll(first, HALF, 1), second)
    sq_ref[...] = jnp.zeros_like(sq_ref)

    def spread(piece_ref, half, column, scale):
        piece = piece_ref[half * HALF : (half + 1) * HALF, column : column + LANES]
        piece = piece.astype(jnp.float32) * scale
        turned = pltpu.roll(piece, HALF, 1)
        zero = jnp.zeros_like(piece)
        return (
            (jnp.where(low, piece, zero), jnp.where(low, zero, turned)),
            (jnp.where(low, turned, zero), jnp.where(low, zero, piece)),
        )

    def lay(pieces, start):
        count = len(pieces) * HALF
        for place, (which, half) in enumerate(pieces):
            keys = spread(kv_refs[which], half, 0, HD ** -0.5)
            values = spread(kv_refs[which], half, LANES, 1.0)
            for group in range(KVH):
                for parity in range(2):
                    row = start + parity * count + place * HALF
                    kb_ref[group, row : row + HALF, :] = keys[group][parity].astype(jnp.bfloat16)
                    vb_ref[group, row : row + HALF, :] = values[group][parity].astype(jnp.bfloat16)

    def half_of(quad, group, half, pieces, start, lse_half_ref):
        rows = slice(half * HALF, (half + 1) * HALF)
        pair = group * 8 + lax.rem(quad, 4)
        columns = [pl.ds(pl.multiple_of((pair + 4 * i) * LANES, LANES), LANES) for i in range(2)]
        queries = jnp.concatenate([q_ref[rows, c] for c in columns], axis=0)
        prior = jnp.concatenate([prior_ref[rows, c] for c in columns], axis=0)
        count = len(pieces) * HALF
        keys = kb_ref[group, start : start + 2 * count, :]
        values = vb_ref[group, start : start + 2 * count, :]
        scores = dot_t(keys, queries)
        prior_t = dot_t(eye, prior)
        powers, shares = [], []
        for parity in range(2):
            parts = []
            for place, (_, _, rule) in enumerate(pieces):
                row = parity * count + place * HALF
                part = scores[row : row + HALF, :]
                if rule == "tri":
                    ahead = iota((HALF, LANES), 0) > (iota((HALF, LANES), 1) & (HALF - 1))
                    part = jnp.where(ahead, -1e30, part)
                elif rule is not None:
                    part = jnp.where(block == rule, -1e30, part)
                parts.append(part)
            own = jnp.concatenate(parts, axis=0)
            logs = lse_half_ref[pl.ds(group * 8 + 2 * lax.rem(quad, 4) + parity, 1), :]
            top = jnp.maximum(jnp.max(own, axis=0, keepdims=True), logs)
            power = jnp.exp(own - top)
            carried = jnp.exp(logs - top)
            total = carried + jnp.sum(power, axis=0, keepdims=True)
            powers.append(power.astype(jnp.bfloat16))
            shares.append((carried, 1.0 / total))
        mixed = lax.dot_general(
            values, jnp.concatenate(powers, axis=0), (((0,), (0,)), ((), ())),
            preferred_element_type=jnp.float32,
        )
        result = jnp.concatenate(
            [
                (carried * prior_t[p * HALF : (p + 1) * HALF] + mixed[p * HALF : (p + 1) * HALF])
                * inverse
                for p, (carried, inverse) in enumerate(shares)
            ],
            axis=0,
        ).astype(jnp.bfloat16)
        upright = dot_t(eye, result)
        sq_ref[rows, :] += upright[:HALF] * upright[:HALF] + upright[HALF:] * upright[HALF:]
        for i, c in enumerate(columns):
            out_ref[rows, c] = upright[i * HALF : (i + 1) * HALF].astype(jnp.bfloat16)

    def attend(first_half, second_half):
        begin = 2 * HALF * len(first_half)
        lay([piece[:2] for piece in first_half], 0)
        lay([piece[:2] for piece in second_half], begin)

        @pl.loop(0, QUADS)
        def _(quad):
            group = lax.div(quad, 4)
            half_of(quad, group, 0, first_half, 0, lse0_ref)
            half_of(quad, group, 1, second_half, begin, lse1_ref)

    @pl.when(block >= 2)
    def _():
        attend(
            [(0, 0, "tri"), (1, 0, None), (2, 0, None)],
            [(0, 0, None), (0, 1, "tri"), (1, 0, None), (2, 0, None)],
        )

    @pl.when(block < 2)
    def _():
        attend(
            [(0, 0, "tri"), (1, 0, 0)],
            [(0, 0, None), (0, 1, "tri"), (1, 0, None), (1, 1, 1), (2, 0, None), (2, 1, None)],
        )

    mean = jnp.sum(sq_ref[...], axis=-1, keepdims=True) * (1.0 / D)
    inverse = lax.rsqrt(mean + 1e-06)
    normed = (out_ref[...].astype(jnp.float32) * inverse * gain_ref[...]).astype(jnp.bfloat16)

    experts = iota((EXPERTS, TOK), 0)
    chosen = [ids_ref[j : j + 1, :] == experts for j in range(2)]
    named = chosen[0] | chosen[1]
    before = as_bf16(iota((TOK, TOK), 0) < iota((TOK, TOK), 1))
    rank = dot_f32(as_bf16(named), before)
    code = jnp.where(named, rank, -1.0).astype(jnp.bfloat16)
    weights = rw_ref[...].astype(jnp.float32)
    weight = (
        jnp.where(chosen[0], weights[0:1, :], 0.0) + jnp.where(chosen[1], weights[1:2, :], 0.0)
    ).astype(jnp.bfloat16)
    total_rows = EXPERTS * MSG_ROWS
    repeat = as_bf16(iota((total_rows, EXPERTS), 0) // MSG_ROWS == iota((total_rows, EXPERTS), 1))
    codes = dot_f32(repeat, code).astype(jnp.int32)
    place = iota((total_rows, TOK), 0) & (MSG_ROWS - 1)
    picked = codes == place
    main = as_bf16(picked)
    spread_weights = jnp.where(picked, dot_f32(repeat, weight), 0.0).astype(jnp.bfloat16)
    send_ref[:, MAIN:] = dot_f32(
        spread_weights, jnp.ones((TOK, LANES), jnp.bfloat16)
    ).astype(jnp.bfloat16)
    last = normed[:, MAIN:]
    for k in range(3):
        wanted = jnp.where(place == 6, k, jnp.where(place == 7, 3 + k, -2))
        select = jnp.concatenate([main, as_bf16(codes == wanted)], axis=1)
        columns = slice(k * TAIL, (k + 1) * TAIL)
        rows = jnp.concatenate([normed[:, columns], last], axis=0)
        send_ref[:, columns] = dot_f32(select, rows).astype(jnp.bfloat16)


def attend_and_pack(query, blocks, prior, logs, gain, ids, weights):
    vmem = pl.BlockSpec(memory_space=pltpu.VMEM)
    return pl.pallas_call(
        attend_kernel,
        out_shape=(
            jax.ShapeDtypeStruct((TOK, D), jnp.bfloat16),
            jax.ShapeDtypeStruct((EXPERTS * MSG_ROWS, PAYLOAD), jnp.bfloat16),
        ),
        in_specs=[vmem] * 9,
        out_specs=(vmem, vmem),
        scratch_shapes=[
            pltpu.VMEM((KVH, 16 * HALF, LANES), jnp.bfloat16),
            pltpu.VMEM((KVH, 16 * HALF, LANES), jnp.bfloat16),
            pltpu.VMEM((16, LANES), jnp.float32),
            pltpu.VMEM((16, LANES), jnp.float32),
            pltpu.VMEM((TOK, LANES), jnp.float32),
        ],
        cost_estimate=pl.CostEstimate(
            flops=2_000_000_000, bytes_accessed=4_000_000, transcendentals=1_000_000
        ),
        name="attend_and_pack",
    )(query, *blocks, prior, logs, gain, ids, weights)


def expert_kernel(got_ref, gate_ref, up_ref, out_ref, rows_ref, weight_ref):
    step_rows, step_slots = 16 * MSG_ROWS, 16 * CAP
    slot, source = iota((step_slots, step_rows), 0), iota((step_slots, step_rows), 1)
    rank, sender = lax.rem(slot, CAP), lax.div(slot, CAP) * MSG_ROWS
    main = as_bf16(source == sender + rank)
    tails = [
        as_bf16(
            ((rank == k) & (source == sender + 6)) | ((rank == 3 + k) & (source == sender + 7))
        )
        for k in range(3)
    ]
    tail = jnp.concatenate(tails, axis=1)
    for step in range(EXPERTS // 16):
        rows = slice(step * step_rows, (step + 1) * step_rows)
        slots = slice(step * step_slots, (step + 1) * step_slots)
        rows_ref[slots, :MAIN] = dot_f32(main, got_ref[rows, :MAIN]).astype(jnp.bfloat16)
        stacked = jnp.concatenate(
            [got_ref[rows, k * TAIL : (k + 1) * TAIL] for k in range(3)], axis=0
        )
        rows_ref[slots, MAIN:] = dot_f32(tail, stacked).astype(jnp.bfloat16)
        weight_ref[slots, :] = dot_f32(main, got_ref[rows, MAIN:])

    width = 256

    @pl.loop(0, FF // width)
    def _(tile):
        columns = pl.ds(pl.multiple_of(tile * width, width), width)
        gate = dot_f32(rows_ref[...], gate_ref[:, columns])
        up = dot_f32(rows_ref[...], up_ref[:, columns])
        weight = weight_ref[...]
        weight = jnp.concatenate([weight] * (width // LANES), axis=1)
        out_ref[:, columns] = (jax.nn.silu(gate) * up * weight).astype(jnp.bfloat16)


def expert_rows(got, w_gate, w_up):
    vmem = pl.BlockSpec(memory_space=pltpu.VMEM)
    return pl.pallas_call(
        expert_kernel,
        out_shape=jax.ShapeDtypeStruct((EXPERTS * CAP, FF), jnp.bfloat16),
        in_specs=[vmem] * 3,
        out_specs=vmem,
        scratch_shapes=[
            pltpu.VMEM((EXPERTS * CAP, D), jnp.bfloat16),
            pltpu.VMEM((EXPERTS * CAP, LANES), jnp.float32),
        ],
        cost_estimate=pl.CostEstimate(
            flops=2_600_000_000, bytes_accessed=9_000_000, transcendentals=300_000
        ),
        name="expert_rows",
    )(got, w_gate, w_up)


def passed_along(block, distance):
    count = lax.axis_size("ctx")
    route = [((i - distance) % count, i) for i in range(count)]
    return lax.ppermute(block, "ctx", route)


def per_device(
    query, key_value, prior_out, prior_lse, norm_gain, w_gate, w_up, expert_ids, route_weight
):
    own = key_value[0]
    blocks = (own, passed_along(own, 1), passed_along(own, 2))
    attended, payload = attend_and_pack(
        query[0], blocks, prior_out[0], prior_lse[0].T, norm_gain[None, :],
        expert_ids[0].T, route_weight[0].T,
    )
    got = lax.all_to_all(
        payload.reshape(EXPERTS, MSG_ROWS, PAYLOAD), "exp", split_axis=0, concat_axis=0, tiled=True
    )
    hidden = expert_rows(got.reshape(EXPERTS * MSG_ROWS, PAYLOAD), w_gate[0], w_up[0])
    return attended[None], hidden[None, None]


def solution(mesh):
    placed = (
        P("exp", "ctx", None),
        P("exp", "ctx", None),
        P("exp", "ctx", None),
        P("exp", "ctx", None),
        P(),
        P("exp", None, None),
        P("exp", None, None),
        P("exp", "ctx", None),
        P("exp", "ctx", None),
    )
    return jax.shard_map(
        per_device,
        mesh=mesh,
        in_specs=placed,
        out_specs=(P("exp", "ctx", None), P("ctx", "exp", None, None)),
        check_vma=False,
    )
```

```python
import jax
import jax.numpy as jnp
from jax import lax
from jax.experimental import pallas as pl
from jax.experimental.pallas import tpu as pltpu
from jax.sharding import PartitionSpec as P

HQ = 32
KVH = 2
HD = 64
FF = 768
D = HQ * HD
TOK = 128
HALF = TOK // 2
EXPERTS = 64
CAP = 6
LANES = 128
MSG_ROWS = 8
MAIN = CAP * D // MSG_ROWS
TAIL = D - MAIN
PAYLOAD = MAIN + LANES
LAST_LANES = (((1,), (1,)), ((), ()))
PAIRS = KVH * 8
QUADS = PAIRS // 2


def iota(shape, dim):
    return lax.broadcasted_iota(jnp.int32, shape, dim)


def as_bf16(mask):
    return jnp.where(mask, 1.0, 0.0).astype(jnp.bfloat16)


def dot_f32(a, b):
    return jnp.dot(a, b, preferred_element_type=jnp.float32)


def dot_t(a, b):
    return lax.dot_general(a, b, LAST_LANES, preferred_element_type=jnp.float32)


def spread(piece, scale):
    low = iota((1, LANES), 1) < HD
    piece = piece.astype(jnp.float32) * scale
    turned = pltpu.roll(piece, HD, 1)
    zero = jnp.zeros_like(piece)
    blocks = (
        (jnp.where(low, piece, zero), jnp.where(low, zero, turned)),
        (jnp.where(low, turned, zero), jnp.where(low, zero, piece)),
    )
    return [[block.astype(jnp.bfloat16) for block in pair] for pair in blocks]


def lay(pieces):
    keys = [spread(piece[:, :LANES], HD ** -0.5) for piece in pieces]
    values = [spread(piece[:, LANES:], 1.0) for piece in pieces]

    def stack(blocks, group):
        return jnp.concatenate(
            [block[group][parity] for parity in range(2) for block in blocks], axis=0
        )

    eye = unit()
    return (
        [stack(keys, group) for group in range(KVH)],
        [dot_t(eye, stack(values, group)).astype(jnp.bfloat16) for group in range(KVH)],
    )


def unit():
    return as_bf16(iota((LANES, LANES), 0) == iota((LANES, LANES), 1))


def ahead():
    return iota((HALF, LANES), 0) > (iota((HALF, LANES), 1) & (HALF - 1))


def pairs_of(quad):
    pair = quad // 4 * 8 + quad % 4
    return pair, pair + 4


def both(rows):
    return jnp.concatenate([jnp.broadcast_to(row, (HD, row.shape[1])) for row in rows], axis=0)


def slots(ids, weights, pick_ref, weight_ref):
    experts = iota((EXPERTS, TOK), 0)
    chosen = [ids[j : j + 1, :] == experts for j in range(2)]
    named = chosen[0] | chosen[1]
    before = as_bf16(iota((TOK, TOK), 0) < iota((TOK, TOK), 1))
    rank = dot_f32(as_bf16(named), before)
    code = jnp.where(named, rank, -1.0).astype(jnp.bfloat16)
    weights = weights.astype(jnp.float32)
    weight = (
        jnp.where(chosen[0], weights[0:1, :], 0.0) + jnp.where(chosen[1], weights[1:2, :], 0.0)
    ).astype(jnp.bfloat16)
    both_codes = jnp.concatenate([code, weight], axis=1)
    step = 128
    ones = jnp.ones((TOK, LANES), jnp.bfloat16)
    place = iota((step, TOK), 0) & (MSG_ROWS - 1)
    for start in range(0, EXPERTS * MSG_ROWS, step):
        rows = slice(start, start + step)
        repeat = as_bf16(
            (iota((step, EXPERTS), 0) + start) // MSG_ROWS == iota((step, EXPERTS), 1)
        )
        repeated = dot_f32(repeat, both_codes)
        codes = repeated[:, :TOK].astype(jnp.int32)
        picked = codes == place
        pick_ref[rows, :TOK] = as_bf16(picked)
        carried = jnp.where(picked, repeated[:, TOK:], 0.0).astype(jnp.bfloat16)
        weight_ref[rows, :] = dot_f32(carried, ones).astype(jnp.bfloat16)
        for k in range(3):
            wanted = jnp.where(place == 6, k, jnp.where(place == 7, 3 + k, -2))
            pick_ref[rows, (k + 1) * TOK : (k + 2) * TOK] = as_bf16(codes == wanted)


def front_kernel(
    q_hbm, kv_hbm, prior_hbm, lse_hbm, ids_hbm, rw_hbm,
    qs_ref, mix_ref, top_ref, sum_ref, pick_ref, weight_ref,
    kv_ref, prior_ref, lse_ref, ids_ref, rw_ref, sems,
):
    copies = [
        pltpu.make_async_copy(kv_hbm, kv_ref, sems.at[0]),
        pltpu.make_async_copy(lse_hbm, lse_ref, sems.at[1]),
        pltpu.make_async_copy(ids_hbm, ids_ref, sems.at[2]),
        pltpu.make_async_copy(rw_hbm, rw_ref, sems.at[3]),
    ]
    for copy in copies:
        copy.start()
    moves = []
    for quad in range(QUADS):
        for half in range(2):
            for i, pair in enumerate(pairs_of(quad)):
                rows, columns = slice(half * HALF, (half + 1) * HALF), slice(pair * LANES, (pair + 1) * LANES)
                target = slice(half * LANES + i * HALF, half * LANES + (i + 1) * HALF)
                moves.append(
                    pltpu.make_async_copy(q_hbm.at[rows, columns], qs_ref.at[quad, target, :], sems.at[4])
                )
                moves.append(
                    pltpu.make_async_copy(prior_hbm.at[rows, columns], prior_ref.at[quad, target, :], sems.at[5])
                )
    for move in moves:
        move.start()
    for copy in copies:
        copy.wait()
    slots(ids_ref[...], rw_ref[...], pick_ref, weight_ref)
    keys, values = lay([kv_ref[:HALF, :], kv_ref[HALF:, :]])
    eye = unit()
    low = iota((1, LANES), 1) < HALF
    late = ahead()
    for move in moves:
        move.wait()

    def scores(quad):
        group = quad // 4
        early = jnp.concatenate([keys[group][:HALF], keys[group][2 * HALF : 3 * HALF]], axis=0)
        return (
            dot_t(early, qs_ref[quad, :LANES, :]),
            dot_t(keys[group], qs_ref[quad, LANES:, :]),
        )

    def soften(quad, found):
        group, head = quad // 4, quad // 4 * 16 + 2 * (quad % 4)
        for half in range(2):
            powers, carries = [], []
            for parity in range(2):
                first = lse_ref[head + parity : head + parity + 1, :]
                second = lse_ref[head + parity + 8 : head + parity + 9, :]
                if half == 0:
                    logs = jnp.where(low, first, pltpu.roll(second, HALF, 1))
                    own = found[0][parity * HALF : (parity + 1) * HALF]
                    own = jnp.where(late, -1e30, own)
                else:
                    logs = jnp.where(low, pltpu.roll(first, HALF, 1), second)
                    own = found[1][parity * TOK : (parity + 1) * TOK]
                    own = jnp.concatenate(
                        [own[:HALF], jnp.where(late, -1e30, own[HALF:])], axis=0
                    )
                top = jnp.maximum(jnp.max(own, axis=0, keepdims=True), logs)
                power = jnp.exp(own - top)
                carried = jnp.exp(logs - top)
                row = quad * 4 + half * 2 + parity
                top_ref[row : row + 1, :] = top
                sum_ref[row : row + 1, :] = carried + jnp.sum(power, axis=0, keepdims=True)
                powers.append(power.astype(jnp.bfloat16))
                carries.append(carried)
            turned = values[group]
            if half == 0:
                turned = jnp.concatenate([turned[:, :HALF], turned[:, 2 * HALF : 3 * HALF]], axis=1)
            mixed = dot_f32(turned, jnp.concatenate(powers, axis=0))
            prior = dot_t(eye, prior_ref[quad, half * LANES : (half + 1) * LANES, :])
            mix_ref[quad, :, half * LANES : (half + 1) * LANES] = both(carries) * prior + mixed

    held = scores(0)
    for quad in range(QUADS):
        following = scores(quad + 1) if quad + 1 < QUADS else None
        soften(quad, held)
        held = following


def back_kernel(
    kv1_ref, kv2_ref, qs_ref, mix_ref, top_ref, sum_ref, pick_ref, weight_ref, gain_ref,
    out_ref, send_ref,
):
    block = lax.axis_index("ctx")
    eye = unit()

    def scores_of(keys, quad, tokens):
        return dot_t(keys[quad // 4], qs_ref[quad, tokens, :])

    def soften(quad, found, count, values, tokens, masks):
        powers, scales, inverses = [], [], []
        for parity in range(2):
            new = found[parity * count : (parity + 1) * count]
            if masks:
                new = jnp.concatenate(
                    [
                        part if rule is None else jnp.where(block == rule, -1e30, part)
                        for part, rule in (
                            (new[i * HALF : (i + 1) * HALF], rule) for i, rule in enumerate(masks)
                        )
                    ],
                    axis=0,
                )
            halves = range(tokens.start // LANES, tokens.stop // LANES)
            rows = [quad * 4 + half * 2 + parity for half in halves]
            old = jnp.concatenate([top_ref[row : row + 1, :] for row in rows], axis=1)
            total = jnp.concatenate([sum_ref[row : row + 1, :] for row in rows], axis=1)
            top = jnp.maximum(jnp.max(new, axis=0, keepdims=True), old)
            scale = jnp.exp(old - top)
            power = jnp.exp(new - top)
            total = total * scale + jnp.sum(power, axis=0, keepdims=True)
            powers.append(power.astype(jnp.bfloat16))
            inverse = 1.0 / total
            scales.append(scale * inverse)
            inverses.append(inverse)
        mixed = dot_f32(values[quad // 4], jnp.concatenate(powers, axis=0))
        result = mix_ref[quad, :, tokens] * both(scales) + mixed * both(inverses)
        return result.astype(jnp.bfloat16)

    def finish(quad, result, tokens):
        for place, half in enumerate(range(tokens.start // LANES, tokens.stop // LANES)):
            upright = dot_t(eye, result[:, place * LANES : (place + 1) * LANES])
            for i, pair in enumerate(pairs_of(quad)):
                out_ref[half * HALF : (half + 1) * HALF, pair * LANES : (pair + 1) * LANES] = (
                    upright[i * HALF : (i + 1) * HALF].astype(jnp.bfloat16)
                )

    def run(tasks):
        found, results = {}, {}
        for step in range(len(tasks) + 2):
            if step < len(tasks):
                quad, keys, _, _, tokens, _ = tasks[step]
                found[step] = scores_of(keys, quad, tokens)
            if 1 <= step <= len(tasks):
                quad, _, values, count, tokens, masks = tasks[step - 1]
                results[step - 1] = soften(quad, found.pop(step - 1), count, values, tokens, masks)
            if step >= 2:
                quad, tokens = tasks[step - 2][0], tasks[step - 2][4]
                finish(quad, results.pop(step - 2), tokens)

    @pl.when(block >= 2)
    def _():
        keys, values = lay([kv1_ref[:HALF, :], kv2_ref[:HALF, :]])
        everyone = slice(0, 2 * LANES)
        run([(quad, keys, values, TOK, everyone, None) for quad in range(QUADS)])

    @pl.when(block < 2)
    def _():
        near_keys, near_values = lay([kv1_ref[:HALF, :]])
        all_keys, all_values = lay(
            [kv1_ref[:HALF, :], kv1_ref[HALF:, :], kv2_ref[:HALF, :], kv2_ref[HALF:, :]]
        )
        tasks = []
        for quad in range(QUADS):
            tasks.append((quad, near_keys, near_values, HALF, slice(0, LANES), [0]))
            tasks.append(
                (quad, all_keys, all_values, 4 * HALF, slice(LANES, 2 * LANES), [None, 1, None, None])
            )
        run(tasks)

    squares = jnp.zeros((TOK, LANES), jnp.float32)
    for pair in range(PAIRS):
        value = out_ref[:, pair * LANES : (pair + 1) * LANES].astype(jnp.float32)
        squares += value * value
    inverse = lax.rsqrt(jnp.sum(squares, axis=-1, keepdims=True) * (1.0 / D) + 1e-06)

    def normed(columns):
        value = out_ref[:, columns].astype(jnp.float32)
        return (value * inverse * gain_ref[:, columns]).astype(jnp.bfloat16)

    send_ref[:, MAIN:] = weight_ref[...]
    last = normed(slice(MAIN, D))
    for k in range(3):
        columns = slice(k * TAIL, (k + 1) * TAIL)
        rows = jnp.concatenate([normed(columns), last], axis=0)
        select = jnp.concatenate(
            [pick_ref[:, :TOK], pick_ref[:, (k + 1) * TOK : (k + 2) * TOK]], axis=1
        )
        send_ref[:, columns] = dot_f32(select, rows).astype(jnp.bfloat16)


def front(query, key_value, prior_out, prior_lse, norm_gain, expert_ids, route_weight):
    vmem = pl.BlockSpec(memory_space=pltpu.VMEM)
    hbm = pl.BlockSpec(memory_space=pltpu.HBM)
    own = key_value[0]
    blocks = passed_along(own, 1), passed_along(own, 2)
    rows = EXPERTS * MSG_ROWS
    state = pl.pallas_call(
        front_kernel,
        out_shape=(
            jax.ShapeDtypeStruct((QUADS, 2 * LANES, LANES), jnp.bfloat16),
            jax.ShapeDtypeStruct((QUADS, LANES, 2 * LANES), jnp.float32),
            jax.ShapeDtypeStruct((4 * QUADS, LANES), jnp.float32),
            jax.ShapeDtypeStruct((4 * QUADS, LANES), jnp.float32),
            jax.ShapeDtypeStruct((rows, 4 * TOK), jnp.bfloat16),
            jax.ShapeDtypeStruct((rows, LANES), jnp.bfloat16),
        ),
        in_specs=[hbm] * 6,
        out_specs=(vmem,) * 6,
        scratch_shapes=[
            pltpu.VMEM((TOK, 2 * LANES), jnp.bfloat16),
            pltpu.VMEM((QUADS, 2 * LANES, LANES), jnp.bfloat16),
            pltpu.VMEM((HQ, TOK), jnp.float32),
            pltpu.VMEM((2, TOK), jnp.int32),
            pltpu.VMEM((2, TOK), jnp.bfloat16),
            pltpu.SemaphoreType.DMA((6,)),
        ],
        cost_estimate=pl.CostEstimate(
            flops=1_500_000_000, bytes_accessed=4_000_000, transcendentals=500_000
        ),
        compiler_params=pltpu.CompilerParams(vmem_limit_bytes=12 * 2**20),
        name="front",
    )(
        *(
            pltpu.with_memory_space_constraint(array, pltpu.HBM)
            for array in (
                query[0], own, prior_out[0], prior_lse[0].T, expert_ids[0].T, route_weight[0].T
            )
        )
    )
    return pl.pallas_call(
        back_kernel,
        out_shape=(
            jax.ShapeDtypeStruct((TOK, D), jnp.bfloat16),
            jax.ShapeDtypeStruct((rows, PAYLOAD), jnp.bfloat16),
        ),
        in_specs=[vmem] * 9,
        out_specs=(vmem, vmem),
        cost_estimate=pl.CostEstimate(
            flops=1_500_000_000, bytes_accessed=4_000_000, transcendentals=500_000
        ),
        compiler_params=pltpu.CompilerParams(vmem_limit_bytes=16 * 2**20),
        name="back",
    )(*blocks, *state, norm_gain[None, :])


def expert_kernel(got_ref, gate_ref, up_ref, out_ref, rows_ref, weight_ref):
    step_rows, step_slots = 16 * MSG_ROWS, 16 * CAP
    slot, source = iota((step_slots, step_rows), 0), iota((step_slots, step_rows), 1)
    rank, sender = lax.rem(slot, CAP), lax.div(slot, CAP) * MSG_ROWS
    main = as_bf16(source == sender + rank)
    tails = [
        as_bf16(
            ((rank == k) & (source == sender + 6)) | ((rank == 3 + k) & (source == sender + 7))
        )
        for k in range(3)
    ]
    tail = jnp.concatenate(tails, axis=1)
    for step in range(EXPERTS // 16):
        rows = slice(step * step_rows, (step + 1) * step_rows)
        slots = slice(step * step_slots, (step + 1) * step_slots)
        rows_ref[slots, :MAIN] = dot_f32(main, got_ref[rows, :MAIN]).astype(jnp.bfloat16)
        stacked = jnp.concatenate(
            [got_ref[rows, k * TAIL : (k + 1) * TAIL] for k in range(3)], axis=0
        )
        rows_ref[slots, MAIN:] = dot_f32(tail, stacked).astype(jnp.bfloat16)
        weight_ref[slots, :] = dot_f32(main, got_ref[rows, MAIN:])

    width = 256

    @pl.loop(0, FF // width)
    def _(tile):
        columns = pl.ds(pl.multiple_of(tile * width, width), width)
        gate = dot_f32(rows_ref[...], gate_ref[:, columns])
        up = dot_f32(rows_ref[...], up_ref[:, columns])
        weight = weight_ref[...]
        weight = jnp.concatenate([weight] * (width // LANES), axis=1)
        out_ref[:, columns] = (jax.nn.silu(gate) * up * weight).astype(jnp.bfloat16)


def expert_rows(got, w_gate, w_up):
    vmem = pl.BlockSpec(memory_space=pltpu.VMEM)
    return pl.pallas_call(
        expert_kernel,
        out_shape=jax.ShapeDtypeStruct((EXPERTS * CAP, FF), jnp.bfloat16),
        in_specs=[vmem] * 3,
        out_specs=vmem,
        scratch_shapes=[
            pltpu.VMEM((EXPERTS * CAP, D), jnp.bfloat16),
            pltpu.VMEM((EXPERTS * CAP, LANES), jnp.float32),
        ],
        cost_estimate=pl.CostEstimate(
            flops=2_600_000_000, bytes_accessed=9_000_000, transcendentals=300_000
        ),
        compiler_params=pltpu.CompilerParams(vmem_limit_bytes=20 * 2**20),
        name="expert_rows",
    )(got, w_gate, w_up)


def passed_along(block, distance):
    count = lax.axis_size("ctx")
    route = [((i - distance) % count, i) for i in range(count)]
    return lax.ppermute(block, "ctx", route)


def per_device(
    query, key_value, prior_out, prior_lse, norm_gain, w_gate, w_up, expert_ids, route_weight
):
    attended, payload = front(
        query, key_value, prior_out, prior_lse, norm_gain, expert_ids, route_weight
    )
    got = lax.all_to_all(
        payload.reshape(EXPERTS, MSG_ROWS, PAYLOAD), "exp", split_axis=0, concat_axis=0, tiled=True
    )
    hidden = expert_rows(got.reshape(EXPERTS * MSG_ROWS, PAYLOAD), w_gate[0], w_up[0])
    return attended[None], hidden[None, None]


def solution(mesh):
    placed = (
        P("exp", "ctx", None),
        P("exp", "ctx", None),
        P("exp", "ctx", None),
        P("exp", "ctx", None),
        P(),
        P("exp", None, None),
        P("exp", None, None),
        P("exp", "ctx", None),
        P("exp", "ctx", None),
    )
    return jax.shard_map(
        per_device,
        mesh=mesh,
        in_specs=placed,
        out_specs=(P("exp", "ctx", None), P("ctx", "exp", None, None)),
        check_vma=False,
    )
```

```python
import jax
import jax.numpy as jnp
from jax import lax
from jax.experimental import pallas as pl
from jax.experimental.pallas import tpu as pltpu
from jax.sharding import PartitionSpec as P


HQ = 32
KVH = 2
HD = 64
FF = 768
D = HQ * HD
TOK = 128
HALF = TOK // 2
EXPERTS = 64
CAP = 6
LANES = 128
MSG_ROWS = 8
MAIN = CAP * D // MSG_ROWS
TAIL = D - MAIN
LAST_LANES = (((1,), (1,)), ((), ()))
PAIRS = KVH * 8
QUADS = PAIRS // 2


def iota(shape, dim):
    return lax.broadcasted_iota(jnp.int32, shape, dim)


def as_bf16(mask):
    return jnp.where(mask, 1.0, 0.0).astype(jnp.bfloat16)


def dot_f32(a, b):
    return jnp.dot(a, b, preferred_element_type=jnp.float32)


def dot_t(a, b):
    return lax.dot_general(a, b, LAST_LANES, preferred_element_type=jnp.float32)


def spread(piece, scale):
    low = iota((1, LANES), 1) < HD
    piece = piece.astype(jnp.float32) * scale
    turned = pltpu.roll(piece, HD, 1)
    zero = jnp.zeros_like(piece)
    blocks = (
        (jnp.where(low, piece, zero), jnp.where(low, zero, turned)),
        (jnp.where(low, turned, zero), jnp.where(low, zero, piece)),
    )
    return [[block.astype(jnp.bfloat16) for block in pair] for pair in blocks]


def lay(pieces):
    keys = [spread(piece[:, :LANES], HD ** -0.5) for piece in pieces]
    values = [spread(piece[:, LANES:], 1.0) for piece in pieces]

    def stack(blocks, group):
        return jnp.concatenate(
            [block[group][parity] for parity in range(2) for block in blocks], axis=0
        )

    eye = unit()
    return (
        [stack(keys, group) for group in range(KVH)],
        [dot_t(eye, stack(values, group)).astype(jnp.bfloat16) for group in range(KVH)],
    )


def unit():
    return as_bf16(iota((LANES, LANES), 0) == iota((LANES, LANES), 1))


def ahead():
    return iota((HALF, LANES), 0) > (iota((HALF, LANES), 1) & (HALF - 1))


def pairs_of(quad):
    pair = quad // 4 * 8 + quad % 4
    return pair, pair + 4


def both(rows):
    return jnp.concatenate([jnp.broadcast_to(row, (HD, row.shape[1])) for row in rows], axis=0)


def slots_kernel(ids_ref, rw_ref, pick_ref, weight_ref):
    ids, weights = ids_ref[...], rw_ref[...]
    experts = iota((EXPERTS, TOK), 0)
    chosen = [ids[j : j + 1, :] == experts for j in range(2)]
    named = chosen[0] | chosen[1]
    before = as_bf16(iota((TOK, TOK), 0) < iota((TOK, TOK), 1))
    rank = dot_f32(as_bf16(named), before)
    code = jnp.where(named, rank, -1.0).astype(jnp.bfloat16)
    weights = weights.astype(jnp.float32)
    weight = (
        jnp.where(chosen[0], weights[0:1, :], 0.0) + jnp.where(chosen[1], weights[1:2, :], 0.0)
    ).astype(jnp.bfloat16)
    both_codes = jnp.concatenate([code, weight], axis=1)
    step = 128
    ones = jnp.ones((TOK, LANES), jnp.bfloat16)
    place = iota((step, TOK), 0) & (MSG_ROWS - 1)
    for start in range(0, EXPERTS * MSG_ROWS, step):
        rows = slice(start, start + step)
        repeat = as_bf16(
            (iota((step, EXPERTS), 0) + start) // MSG_ROWS == iota((step, EXPERTS), 1)
        )
        repeated = dot_f32(repeat, both_codes)
        codes = repeated[:, :TOK].astype(jnp.int32)
        picked = codes == place
        pick_ref[rows, :TOK] = as_bf16(picked)
        carried = jnp.where(picked, repeated[:, TOK:], 0.0).astype(jnp.bfloat16)
        weight_ref[rows, :] = dot_f32(carried, ones).astype(jnp.bfloat16)
        for k in range(3):
            wanted = jnp.where(place == 6, k, jnp.where(place == 7, 3 + k, -2))
            pick_ref[rows, (k + 1) * TOK : (k + 2) * TOK] = as_bf16(codes == wanted)


def front_kernel(
    q_hbm, kv_hbm, prior_hbm, lse_hbm,
    qs_ref, mix_ref, top_ref, sum_ref,
    kv_ref, prior_ref, lse_ref, sems,
):
    copies = [
        pltpu.make_async_copy(kv_hbm, kv_ref, sems.at[0]),
        pltpu.make_async_copy(lse_hbm, lse_ref, sems.at[1]),
    ]
    for copy in copies:
        copy.start()
    moves = []
    for quad in range(QUADS):
        for half in range(2):
            for i, pair in enumerate(pairs_of(quad)):
                rows, columns = slice(half * HALF, (half + 1) * HALF), slice(pair * LANES, (pair + 1) * LANES)
                target = slice(half * LANES + i * HALF, half * LANES + (i + 1) * HALF)
                moves.append(
                    pltpu.make_async_copy(q_hbm.at[rows, columns], qs_ref.at[quad, target, :], sems.at[2])
                )
                moves.append(
                    pltpu.make_async_copy(prior_hbm.at[rows, columns], prior_ref.at[quad, target, :], sems.at[3])
                )
    for move in moves:
        move.start()
    for copy in copies:
        copy.wait()
    keys, values = lay([kv_ref[:HALF, :], kv_ref[HALF:, :]])
    eye = unit()
    low = iota((1, LANES), 1) < HALF
    late = ahead()
    for move in moves:
        move.wait()

    def scores(quad):
        group = quad // 4
        early = jnp.concatenate([keys[group][:HALF], keys[group][2 * HALF : 3 * HALF]], axis=0)
        return (
            dot_t(early, qs_ref[quad, :LANES, :]),
            dot_t(keys[group], qs_ref[quad, LANES:, :]),
        )

    def soften(quad, found):
        group, head = quad // 4, quad // 4 * 16 + 2 * (quad % 4)
        for half in range(2):
            powers, carries = [], []
            for parity in range(2):
                first = lse_ref[head + parity : head + parity + 1, :]
                second = lse_ref[head + parity + 8 : head + parity + 9, :]
                if half == 0:
                    logs = jnp.where(low, first, pltpu.roll(second, HALF, 1))
                    own = found[0][parity * HALF : (parity + 1) * HALF]
                    own = jnp.where(late, -1e30, own)
                else:
                    logs = jnp.where(low, pltpu.roll(first, HALF, 1), second)
                    own = found[1][parity * TOK : (parity + 1) * TOK]
                    own = jnp.concatenate(
                        [own[:HALF], jnp.where(late, -1e30, own[HALF:])], axis=0
                    )
                top = jnp.maximum(jnp.max(own, axis=0, keepdims=True), logs)
                power = jnp.exp(own - top)
                carried = jnp.exp(logs - top)
                row = quad * 4 + half * 2 + parity
                top_ref[row : row + 1, :] = top
                sum_ref[row : row + 1, :] = carried + jnp.sum(power, axis=0, keepdims=True)
                powers.append(power.astype(jnp.bfloat16))
                carries.append(carried)
            turned = values[group]
            if half == 0:
                turned = jnp.concatenate([turned[:, :HALF], turned[:, 2 * HALF : 3 * HALF]], axis=1)
            mixed = dot_f32(turned, jnp.concatenate(powers, axis=0))
            prior = dot_t(eye, prior_ref[quad, half * LANES : (half + 1) * LANES, :])
            mix_ref[quad, :, half * LANES : (half + 1) * LANES] = both(carries) * prior + mixed

    held = scores(0)
    for quad in range(QUADS):
        following = scores(quad + 1) if quad + 1 < QUADS else None
        soften(quad, held)
        held = following


def back_kernel(
    kv1_ref, kv2_ref, qs_ref, mix_ref, top_ref, sum_ref, pick_ref, gain_ref,
    out_ref, send_ref,
):
    block = lax.axis_index("ctx")
    eye = unit()

    def scores_of(keys, quad, tokens):
        return dot_t(keys[quad // 4], qs_ref[quad, tokens, :])

    def soften(quad, found, count, values, tokens, masks):
        powers, scales, inverses = [], [], []
        for parity in range(2):
            new = found[parity * count : (parity + 1) * count]
            if masks:
                new = jnp.concatenate(
                    [
                        part if rule is None else jnp.where(block == rule, -1e30, part)
                        for part, rule in (
                            (new[i * HALF : (i + 1) * HALF], rule) for i, rule in enumerate(masks)
                        )
                    ],
                    axis=0,
                )
            halves = range(tokens.start // LANES, tokens.stop // LANES)
            rows = [quad * 4 + half * 2 + parity for half in halves]
            old = jnp.concatenate([top_ref[row : row + 1, :] for row in rows], axis=1)
            total = jnp.concatenate([sum_ref[row : row + 1, :] for row in rows], axis=1)
            top = jnp.maximum(jnp.max(new, axis=0, keepdims=True), old)
            scale = jnp.exp(old - top)
            power = jnp.exp(new - top)
            total = total * scale + jnp.sum(power, axis=0, keepdims=True)
            powers.append(power.astype(jnp.bfloat16))
            inverse = 1.0 / total
            scales.append(scale * inverse)
            inverses.append(inverse)
        mixed = dot_f32(values[quad // 4], jnp.concatenate(powers, axis=0))
        result = mix_ref[quad, :, tokens] * both(scales) + mixed * both(inverses)
        return result.astype(jnp.bfloat16)

    def finish(quad, result, tokens):
        for place, half in enumerate(range(tokens.start // LANES, tokens.stop // LANES)):
            upright = dot_t(eye, result[:, place * LANES : (place + 1) * LANES])
            for i, pair in enumerate(pairs_of(quad)):
                out_ref[half * HALF : (half + 1) * HALF, pair * LANES : (pair + 1) * LANES] = (
                    upright[i * HALF : (i + 1) * HALF].astype(jnp.bfloat16)
                )

    def run(tasks):
        found, results = {}, {}
        for step in range(len(tasks) + 2):
            if step < len(tasks):
                quad, keys, _, _, tokens, _ = tasks[step]
                found[step] = scores_of(keys, quad, tokens)
            if 1 <= step <= len(tasks):
                quad, _, values, count, tokens, masks = tasks[step - 1]
                results[step - 1] = soften(quad, found.pop(step - 1), count, values, tokens, masks)
            if step >= 2:
                quad, tokens = tasks[step - 2][0], tasks[step - 2][4]
                finish(quad, results.pop(step - 2), tokens)

    @pl.when(block >= 2)
    def _():
        keys, values = lay([kv1_ref[:HALF, :], kv2_ref[:HALF, :]])
        everyone = slice(0, 2 * LANES)
        run([(quad, keys, values, TOK, everyone, None) for quad in range(QUADS)])

    @pl.when(block < 2)
    def _():
        near_keys, near_values = lay([kv1_ref[:HALF, :]])
        all_keys, all_values = lay(
            [kv1_ref[:HALF, :], kv1_ref[HALF:, :], kv2_ref[:HALF, :], kv2_ref[HALF:, :]]
        )
        tasks = []
        for quad in range(QUADS):
            tasks.append((quad, near_keys, near_values, HALF, slice(0, LANES), [0]))
            tasks.append(
                (quad, all_keys, all_values, 4 * HALF, slice(LANES, 2 * LANES), [None, 1, None, None])
            )
        run(tasks)

    squares = jnp.zeros((TOK, LANES), jnp.float32)
    for pair in range(PAIRS):
        value = out_ref[:, pair * LANES : (pair + 1) * LANES].astype(jnp.float32)
        squares += value * value
    inverse = lax.rsqrt(jnp.sum(squares, axis=-1, keepdims=True) * (1.0 / D) + 1e-06)

    def normed(columns):
        value = out_ref[:, columns].astype(jnp.float32)
        return (value * inverse * gain_ref[:, columns]).astype(jnp.bfloat16)

    last = normed(slice(MAIN, D))
    for k in range(3):
        columns = slice(k * TAIL, (k + 1) * TAIL)
        rows = jnp.concatenate([normed(columns), last], axis=0)
        select = jnp.concatenate(
            [pick_ref[:, :TOK], pick_ref[:, (k + 1) * TOK : (k + 2) * TOK]], axis=1
        )
        send_ref[:, columns] = dot_f32(select, rows).astype(jnp.bfloat16)


def front(query, key_value, prior_out, prior_lse, norm_gain, expert_ids, route_weight):
    vmem = pl.BlockSpec(memory_space=pltpu.VMEM)
    hbm = pl.BlockSpec(memory_space=pltpu.HBM)
    own = key_value[0]
    first = passed_along(own, 1)
    second = passed_along(own, 2)
    rows = EXPERTS * MSG_ROWS
    pick, weights = pl.pallas_call(
        slots_kernel,
        out_shape=(
            jax.ShapeDtypeStruct((rows, 4 * TOK), jnp.bfloat16),
            jax.ShapeDtypeStruct((rows, LANES), jnp.bfloat16),
        ),
        in_specs=[vmem] * 2,
        out_specs=(vmem,) * 2,
        cost_estimate=pl.CostEstimate(
            flops=100_000_000, bytes_accessed=700_000, transcendentals=0
        ),
        name="slots",
    )(expert_ids[0].T, route_weight[0].T)
    arrived = to_experts(weights)
    state = front_call(query, own, prior_out, prior_lse)
    attended, payload = pl.pallas_call(
        back_kernel,
        out_shape=(
            jax.ShapeDtypeStruct((TOK, D), jnp.bfloat16),
            jax.ShapeDtypeStruct((rows, MAIN), jnp.bfloat16),
        ),
        in_specs=[vmem] * 8,
        out_specs=(vmem, vmem),
        cost_estimate=pl.CostEstimate(
            flops=1_500_000_000, bytes_accessed=4_000_000, transcendentals=500_000
        ),
        compiler_params=pltpu.CompilerParams(vmem_limit_bytes=16 * 2**20),
        name="back",
    )(first, second, *state, pick, norm_gain[None, :])
    return attended, payload, arrived


def front_call(query, own, prior_out, prior_lse):
    vmem = pl.BlockSpec(memory_space=pltpu.VMEM)
    hbm = pl.BlockSpec(memory_space=pltpu.HBM)
    return pl.pallas_call(
        front_kernel,
        out_shape=(
            jax.ShapeDtypeStruct((QUADS, 2 * LANES, LANES), jnp.bfloat16),
            jax.ShapeDtypeStruct((QUADS, LANES, 2 * LANES), jnp.float32),
            jax.ShapeDtypeStruct((4 * QUADS, LANES), jnp.float32),
            jax.ShapeDtypeStruct((4 * QUADS, LANES), jnp.float32),
        ),
        in_specs=[hbm] * 4,
        out_specs=(vmem,) * 4,
        scratch_shapes=[
            pltpu.VMEM((TOK, 2 * LANES), jnp.bfloat16),
            pltpu.VMEM((QUADS, 2 * LANES, LANES), jnp.bfloat16),
            pltpu.VMEM((HQ, TOK), jnp.float32),
            pltpu.SemaphoreType.DMA((4,)),
        ],
        cost_estimate=pl.CostEstimate(
            flops=1_500_000_000, bytes_accessed=4_000_000, transcendentals=500_000
        ),
        compiler_params=pltpu.CompilerParams(vmem_limit_bytes=12 * 2**20),
        name="front",
    )(
        *(
            pltpu.with_memory_space_constraint(array, pltpu.HBM)
            for array in (
                query[0], own, prior_out[0], prior_lse[0].T
            )
        )
    )


def to_experts(rows):
    parts = rows.reshape(EXPERTS, MSG_ROWS, rows.shape[-1])
    parts = lax.all_to_all(parts, "exp", split_axis=0, concat_axis=0, tiled=True)
    return parts.reshape(rows.shape)


def expert_kernel(
    got_ref, sent_ref, gate_ref, up_hbm, out_ref, rows_ref, weight_ref, up_ref, gated_ref, sem
):
    copy = pltpu.make_async_copy(up_hbm, up_ref, sem)
    copy.start()
    step_rows, step_slots = 16 * MSG_ROWS, 16 * CAP
    slot, source = iota((step_slots, step_rows), 0), iota((step_slots, step_rows), 1)
    rank, sender = lax.rem(slot, CAP), lax.div(slot, CAP) * MSG_ROWS
    main = as_bf16(source == sender + rank)
    tails = [
        as_bf16(
            ((rank == k) & (source == sender + 6)) | ((rank == 3 + k) & (source == sender + 7))
        )
        for k in range(3)
    ]
    tail = jnp.concatenate(tails, axis=1)
    for step in range(EXPERTS // 16):
        rows = slice(step * step_rows, (step + 1) * step_rows)
        slots = slice(step * step_slots, (step + 1) * step_slots)
        rows_ref[slots, :MAIN] = dot_f32(main, got_ref[rows, :MAIN]).astype(jnp.bfloat16)
        stacked = jnp.concatenate(
            [got_ref[rows, k * TAIL : (k + 1) * TAIL] for k in range(3)], axis=0
        )
        rows_ref[slots, MAIN:] = dot_f32(tail, stacked).astype(jnp.bfloat16)
        weight_ref[slots, :] = dot_f32(main, sent_ref[rows, :])

    width = 256

    def columns_of(tile):
        return pl.ds(pl.multiple_of(tile * width, width), width)

    @pl.loop(0, FF // width)
    def _(tile):
        columns = columns_of(tile)
        weight = jnp.concatenate([weight_ref[...]] * (width // LANES), axis=1)
        gated_ref[:, columns] = jax.nn.silu(dot_f32(rows_ref[...], gate_ref[:, columns])) * weight

    copy.wait()

    @pl.loop(0, FF // width)
    def _(tile):
        columns = columns_of(tile)
        up = dot_f32(rows_ref[...], up_ref[:, columns])
        out_ref[:, columns] = (gated_ref[:, columns] * up).astype(jnp.bfloat16)


def expert_rows(got, sent, w_gate, w_up):
    vmem = pl.BlockSpec(memory_space=pltpu.VMEM)
    return pl.pallas_call(
        expert_kernel,
        out_shape=jax.ShapeDtypeStruct((EXPERTS * CAP, FF), jnp.bfloat16),
        in_specs=[vmem, vmem, vmem, pl.BlockSpec(memory_space=pltpu.HBM)],
        out_specs=vmem,
        scratch_shapes=[
            pltpu.VMEM((EXPERTS * CAP, D), jnp.bfloat16),
            pltpu.VMEM((EXPERTS * CAP, LANES), jnp.float32),
            pltpu.VMEM((D, FF), jnp.bfloat16),
            pltpu.VMEM((EXPERTS * CAP, FF), jnp.float32),
            pltpu.SemaphoreType.DMA,
        ],
        cost_estimate=pl.CostEstimate(
            flops=2_600_000_000, bytes_accessed=9_000_000, transcendentals=300_000
        ),
        compiler_params=pltpu.CompilerParams(vmem_limit_bytes=20 * 2**20),
        name="expert_rows",
    )(got, sent, w_gate, pltpu.with_memory_space_constraint(w_up, pltpu.HBM))


def passed_along(block, distance):
    count = lax.axis_size("ctx")
    route = [((i - distance) % count, i) for i in range(count)]
    return lax.ppermute(block, "ctx", route)


def per_device(
    query, key_value, prior_out, prior_lse, norm_gain, w_gate, w_up, expert_ids, route_weight
):
    attended, payload, weights = front(
        query, key_value, prior_out, prior_lse, norm_gain, expert_ids, route_weight
    )
    hidden = expert_rows(to_experts(payload), weights, w_gate[0], w_up[0])
    return attended[None], hidden[None, None]


def solution(mesh):
    placed = (
        P("exp", "ctx", None),
        P("exp", "ctx", None),
        P("exp", "ctx", None),
        P("exp", "ctx", None),
        P(),
        P("exp", None, None),
        P("exp", None, None),
        P("exp", "ctx", None),
        P("exp", "ctx", None),
    )
    return jax.shard_map(
        per_device,
        mesh=mesh,
        in_specs=placed,
        out_specs=(P("exp", "ctx", None), P("ctx", "exp", None, None)),
        check_vma=False,
    )
```
